512 devices in a mesh: ctx: 64 (over y, z), ch: 8 (over x, core).
Axes of the slice: x: 4, y: 4, z: 16, core: 2. Of those that a mesh axis runs over, the one named last changes fastest.
Arguments:
- attn_proj: bfloat16 [8704, 3, 2048], P('ctx', None, 'ch'), may hold values from -40 to 40, as said below
- first_in: bfloat16 [8704, 3, 4096], P('ctx', None, 'ch'), may hold values from -6 to 6
- second_in: bfloat16 [8704, 3, 4096], P('ctx', None, 'ch'), may hold values from -6 to 6
- third_in: bfloat16 [8704, 3, 4096], P('ctx', None, 'ch'), may hold values from -6 to 6
- feat_filters: bfloat16 [3, 3, 3, 4096], P(None, None, None, 'ch'), may hold values from -3.5 to 3.5
- short_filters: bfloat16 [2, 7, 256], P(None, None, 'ch'), may hold values from -2 to 2
- long_filter: bfloat16 [128, 256], P('ch'), may hold values from -0.5 to 0.5
- positions: int32 [8704], P('ctx'), may hold values from 0 to 17406, as said below
Outputs:
- attn_out: bfloat16 [8704, 2048], P('ctx', 'ch')
- out_first: bfloat16 [8704, 4096], P('ctx', 'ch')
- out_second: bfloat16 [8704, 4096], P('ctx', 'ch')
- out_third: bfloat16 [8704, 4096], P('ctx', 'ch')
The draws below stay inside these ranges and needn't reach their ends.
Inputs may be any that keep to these rules, and one draw needn't show every extreme that they name: `positions`: each token's position in its packed document: it rises by one from token to token and restarts at 0 at one to three tokens of the slice; the first token's value is how far its document began before the slice, at least 8704. `attn_proj`: entries of order one, except, in some draws, rows whose queries or keys are large.
All inputs are finite; a program needn't handle non-finite values.
Results may differ from the reference program's by a relative error of at most 0.0049.
Values may be sent and summed in bfloat16 or wider, within the bound.
A program may use at most 128 MiB of HBM per device.

```python
import math
import jax
import jax.numpy as jnp
from jax import lax

D = 4096
HD = 128
ATT_HEADS = 16
GROUP = 16
FEAT_TAPS = 3
SHORT_TAPS = 7
LONG_TAPS = 128
TOKENS = 8704


def draw_attn_proj(key, part):
    channels = ATT_HEADS * HD
    key_base = jax.random.fold_in(key, 11)
    background = jnp.clip(jax.random.normal(key_base, (TOKENS, 3, channels), jnp.float32), -6.0, 6.0)
    return background.astype(jnp.bfloat16)


def draw_positions(key, part):
    key_cuts = jax.random.fold_in(key, 21)
    cut_points = jax.random.randint(key_cuts, (3,), 1, TOKENS, dtype=jnp.int32)
    first_cut = jnp.min(cut_points)
    lead_offset = (2 * TOKENS - 1 - first_cut).astype(jnp.int32)
    row_ids = jnp.arange(TOKENS, dtype=jnp.int32)
    starts = jnp.where(cut_points[None, :] <= row_ids[:, None], cut_points[None, :], -lead_offset)
    latest = jnp.max(starts, axis=1)
    return (row_ids - latest).astype(jnp.int32)


def level_of(rng, extent, shards, least, top_value):
    level, own = 1.0, jax.random.fold_in(rng, 6)
    for axis_at, shards_of in shards:
        steps = jnp.exp(jax.random.uniform(jax.random.fold_in(own, axis_at), (shards_of,), jnp.float32, least / len(shards), top_value / len(shards)))
        level = level * jnp.repeat(steps, extent[axis_at] // shards_of).reshape([-1 if axis == axis_at else 1 for axis in range(len(extent))])
    return level


def gaussian(key, shape, spread, reach, pieces=(), held_as=jnp.bfloat16):
    entries = spread * jax.random.normal(key, shape, jnp.float32)
    if pieces:
        entries = entries * level_of(key, shape, pieces, -0.22, 0.18)
    return jnp.clip(entries, -reach, reach).astype(held_as)


def setup_inputs(seed: int = 0) -> dict:
    seeds = jax.random.split(jax.random.key(seed), 9)
    return {
        "attn_proj": draw_attn_proj(jax.random.fold_in(seeds[8], 71), 0),
        "first_in": gaussian(seeds[1], (TOKENS, 3, D), 1.0, 6.0, ((0, 64), (2, 8))),
        "second_in": gaussian(seeds[2], (TOKENS, 3, D), 1.0, 6.0, ((0, 64), (2, 8))),
        "third_in": gaussian(seeds[3], (TOKENS, 3, D), 1.0, 6.0, ((0, 64), (2, 8))),
        "feat_filters": gaussian(seeds[4], (3, FEAT_TAPS, 3, D), FEAT_TAPS ** -0.5, 3.5, ((3, 8),)),
        "short_filters": gaussian(seeds[5], (2, SHORT_TAPS, D // GROUP), SHORT_TAPS ** -0.5, 2.0, ((2, 8),)),
        "long_filter": gaussian(seeds[6], (LONG_TAPS, D // GROUP), LONG_TAPS ** -0.5, 0.5, ((0, 8),)),
        "positions": draw_positions(jax.random.fold_in(seeds[8], 71), 0),
    }


def lagged_sum(values, filters, positions):
    tap_count = filters.shape[0]
    row_count = values.shape[0]
    padded = jnp.pad(values, ((tap_count - 1, 0), (0, 0)))

    def add_lag(offset, summed):
        shifted = lax.dynamic_slice_in_dim(padded, tap_count - 1 - offset, row_count, 0)
        in_doc = (offset <= positions).astype(jnp.float32)[:, None]
        return summed + in_doc * filters[offset][None, :] * shifted
    return lax.fori_loop(0, tap_count, add_lag, jnp.zeros(values.shape, jnp.float32))

def hyena_layer(layer_in, feat_filter, inner_filter, positions):
    row_count = layer_in.shape[0]
    wide_in = layer_in.reshape(row_count, 3 * D).astype(jnp.float32)
    wide_filter = feat_filter.reshape(FEAT_TAPS, 3 * D).astype(jnp.float32)
    featured = lagged_sum(wide_in, wide_filter, positions)
    outer_gate = featured[:, :D]
    mixed_rows = (featured[:, D:2 * D] * featured[:, 2 * D:]).astype(jnp.bfloat16)
    expanded = jnp.repeat(inner_filter.astype(jnp.float32), GROUP, axis=1)
    convolved = lagged_sum(mixed_rows.astype(jnp.float32), expanded, positions)
    return (outer_gate * convolved).astype(jnp.bfloat16)

def attention(attn_proj, positions):
    channels = ATT_HEADS * HD
    queries = attn_proj[:, 0].reshape(TOKENS, ATT_HEADS, HD).astype(jnp.float32)
    key_rows = attn_proj[:, 1].reshape(TOKENS, ATT_HEADS, HD).astype(jnp.float32)
    value_rows = attn_proj[:, 2].reshape(TOKENS, ATT_HEADS, HD).astype(jnp.float32)
    row_ids = jnp.arange(TOKENS, dtype=jnp.int32)
    doc_start = row_ids - positions
    score_scale = 1.0 / math.sqrt(HD)
    block_rows = math.gcd(TOKENS, 256)

    def one_block(block_index):
        first_row = (block_index * block_rows).astype(jnp.int32)
        query_block = lax.dynamic_slice_in_dim(queries, first_row, block_rows, 0)
        query_rows = first_row + jnp.arange(block_rows, dtype=jnp.int32)
        block_start = lax.dynamic_slice_in_dim(doc_start, first_row, block_rows, 0)
        scores = jnp.einsum('thd,shd->hts', query_block, key_rows) * score_scale
        allowed = (row_ids[None, :] <= query_rows[:, None]) & (row_ids[None, :] >= block_start[:, None])
        scores = jnp.where(allowed[None], scores, -1e+30)
        row_peak = lax.optimization_barrier(jnp.max(scores, axis=-1, keepdims=True))
        weights = jnp.where(allowed[None], jnp.exp(scores - row_peak), 0.0)
        denominator = lax.optimization_barrier(jnp.sum(weights, axis=-1))
        rounded = lax.optimization_barrier(weights.astype(jnp.bfloat16)).astype(jnp.float32)
        result = jnp.einsum('hts,shd->htd', rounded, value_rows) / denominator[:, :, None]
        return jnp.transpose(result, (1, 0, 2)).astype(jnp.bfloat16).reshape(block_rows, channels)
    blocks = lax.map(one_block, jnp.arange(TOKENS // block_rows, dtype=jnp.int32))
    return blocks.reshape(TOKENS, channels)

def reference(attn_proj, first_in, second_in, third_in, feat_filters, short_filters, long_filter, positions):
    attn_out = attention(attn_proj, positions)
    out_first = hyena_layer(first_in, feat_filters[0], short_filters[0], positions)
    out_second = hyena_layer(second_in, feat_filters[1], short_filters[1], positions)
    out_third = hyena_layer(third_in, feat_filters[2], long_filter, positions)
    return (attn_out, out_first, out_second, out_third)
```

```python
import functools
import math

import jax
import jax.numpy as jnp
from jax import lax
from jax.experimental import pallas as pl
from jax.experimental.pallas import tpu as pltpu
from jax.sharding import PartitionSpec as P

NY, NZ, NCH = 4, 16, 8
ROWS = 136
HD = 128
QW = 640
COEF = math.log2(math.e) / math.sqrt(HD)
MESH = pl.DeviceIdType.MESH
BF, F32 = jnp.bfloat16, jnp.float32
TILES = ((0, 256), (256, 256), (512, 128))


def iota(shape, dim):
    return lax.broadcasted_iota(jnp.int32, shape, dim)


def kernel(
    qkv, x0, x1, x2, wf, sf, lf, posl, posc,
    attn, out0, out1, out2,
    qb, kv, pv, xv, rim, lfb, xf, mx, mx2, gate, ml, msend, rimm, mT, cT, cg, erev,
    qall, acc, mrow, lrow, tq, ds, of32, ob, orecv, auxs, auxr,
    loc, ksend, krecv, qsend, qrecv, psend, precv, rsend, rrecv, fsend, frecv,
    mssem, mrsem, osend, osrecv, asend, arecv,
):
    me = lax.axis_index("ctx")
    ch = lax.axis_index("ch")
    y, z = me // NZ, me % NZ
    xs = (x0, x1, x2)

    def zdev(k):
        return y * NZ + (z + k + NZ) % NZ

    def ydev(k):
        return ((y + k) % NY) * NZ + z

    nxt, prv = (me + 1) % (NY * NZ), (me + NY * NZ - 1) % (NY * NZ)

    def rcopy(src, dst, ss, rs, **dev):
        return pltpu.make_async_remote_copy(
            src_ref=src, dst_ref=dst, send_sem=ss, recv_sem=rs, device_id=dev, device_id_type=MESH
        )

    locals_ = [
        pltpu.make_async_copy(qkv.at[pl.ds(1, 2)], kv.at[z], loc.at[0]),
        pltpu.make_async_copy(qkv.at[0], qb.at[0], loc.at[1]),
        pltpu.make_async_copy(posl.at[0], pv.at[0], loc.at[2]),
        pltpu.make_async_copy(lf, lfb.at[ch], loc.at[3]),
    ] + [pltpu.make_async_copy(xs[i], xv.at[i], loc.at[4 + i]) for i in range(3)]
    for c in locals_:
        c.start()

    bar = pltpu.get_barrier_semaphore()
    peers = [zdev(1), zdev(-1), ydev(1), ydev(2), ydev(3), nxt, prv]
    for p in peers:
        pl.semaphore_signal(bar, inc=1, device_id={"ctx": p}, device_id_type=MESH)
    for d in range(1, NCH):
        pl.semaphore_signal(bar, inc=1, device_id={"ch": (ch + d) % NCH}, device_id_type=MESH)
    pl.semaphore_wait(bar, len(peers) + NCH - 1)

    def kvcopy(d, s, c):
        blk = (z - s + 1 + NZ) % NZ if d == 0 else (z + s - 1) % NZ
        tgt = zdev(1) if d == 0 else zdev(-1)
        return rcopy(kv.at[blk, c], kv.at[blk, c], ksend.at[d, s - 1, c], krecv.at[d, s - 1, c], ctx=tgt)

    def kvwait(d, s, c):
        blk = (z - s + NZ) % NZ if d == 0 else (z + s) % NZ
        rcopy(kv.at[blk, c], kv.at[blk, c], ksend.at[d, s - 1, c], krecv.at[d, s - 1, c], ctx=prv).wait_recv()

    locals_[0].wait()
    for c in range(2):
        for d in range(2):
            kvcopy(d, 1, c).start()
    raw = [rcopy(xs[i].at[:, pl.ds(128, 8), :], rim.at[i], rsend.at[i], rrecv.at[i], ctx=nxt) for i in range(3)]
    for i in (2, 0, 1):
        raw[i].start()
    locals_[1].wait()
    locals_[2].wait()
    locals_[3].wait()
    qs = [rcopy(qb.at[0], qb.at[r], qsend.at[r - 1], qrecv.at[r - 1], ctx=ydev(4 - r)) for r in range(1, 4)]
    ps = [rcopy(posl.at[r], pv.at[r], psend.at[r - 1], precv.at[r - 1], ctx=ydev(4 - r)) for r in range(1, 4)]
    fs = [
        rcopy(lfb.at[ch], lfb.at[ch], fsend.at[d - 1], frecv.at[d - 1], ch=(ch + d) % NCH)
        for d in range(1, NCH)
    ]
    for c in qs + ps + fs:
        c.start()
    for i in range(3):
        locals_[4 + i].wait()

    acc[...] = jnp.zeros_like(acc)
    mrow[...] = jnp.full_like(mrow, -1e20)
    lrow[...] = jnp.zeros_like(lrow)

    for c in qs + ps:
        c.wait_recv()
    lane = iota((8, QW), 1)
    b = (
        (lane >= ROWS).astype(jnp.int32)
        + (lane >= 2 * ROWS).astype(jnp.int32)
        + (lane >= 3 * ROWS).astype(jnp.int32)
    )
    yq = (y + b) % NY
    t_all = (yq * NZ + z) * ROWS + lane - ROWS * b
    tq[...] = t_all
    ds[...] = t_all - (pv[0] + pv[1] + pv[2] + pv[3])
    of32[pl.ds(544, 96), :] = jnp.zeros((96, 256), F32)
    for r in range(4):
        of32[pl.ds(ROWS * r, ROWS), :] = qb[r].astype(F32)
    qall[...] = of32[...].astype(BF)

    def att(blocks):
        for h in range(2):
            hs = pl.ds(h * HD, HD)
            ks = [kv[blk, 0, :, hs] for blk in blocks]
            vs = [kv[blk, 1, :, hs] for blk in blocks]
            for lo, w in TILES:
                cs = pl.ds(lo, w)
                q = qall[cs, hs]
                t_row, d_row = tq[0:1, cs], ds[0:1, cs]
                scores = []
                m_old = mrow[h : h + 1, cs]
                m_new = m_old
                for blk, k in zip(blocks, ks):
                    s = lax.dot_general(k, q, (((1,), (1,)), ((), ())), preferred_element_type=F32)
                    kid = (y * NZ + blk) * ROWS + iota((ROWS, w), 0)
                    s = jnp.where((kid <= t_row) & (kid >= d_row), s, -1e30)
                    scores.append(s)
                    m_new = jnp.maximum(m_new, jnp.max(s, axis=0, keepdims=True))
                alpha = jnp.exp2((m_old - m_new) * COEF)
                l_new = lrow[h : h + 1, cs] * alpha
                o_new = acc[h, :, cs] * alpha
                for s, v in zip(scores, vs):
                    p = jnp.exp2((s - m_new) * COEF)
                    l_new = l_new + jnp.sum(p, axis=0, keepdims=True)
                    o_new = o_new + lax.dot_general(
                        v, p.astype(BF), (((0,), (0,)), ((), ())), preferred_element_type=F32
                    )
                mrow[h : h + 1, cs] = m_new
                lrow[h : h + 1, cs] = l_new
                acc[h, :, cs] = o_new

    def features(i, lanes):
        out = []
        pos = posc[pl.ds(8, 144), :]
        for a in range(3):
            xf[a, pl.ds(0, 8), :] = jnp.zeros((8, 128), F32)
            xf[a, pl.ds(8, 8), :] = jnp.where(me > 0, rim[i, a, :, lanes].astype(F32), 0.0)
            xf[a, pl.ds(16, ROWS), :] = xv[i, a, :, lanes].astype(F32)
            tot = jnp.zeros((144, 128), F32)
            for j in range(3):
                row = (i * 3 + j) * 3 + a
                term = wf[row : row + 1, lanes] * xf[a, pl.ds(8 - j, 144), :]
                tot = tot + (jnp.where(pos >= j, term, 0.0) if j else term)
            out.append(tot)
        mixed = (out[1] * out[2]).astype(BF).astype(F32)
        return out[0][8:], mixed

    def lanes_of(lt):
        return pl.ds(pl.multiple_of(lt * 128, 128), 128)

    def short_layer(i, out):
        def unit(lt, carry):
            lanes = lanes_of(lt)
            g, mixed = features(i, lanes)
            mx[...] = mixed
            pos = posc[pl.ds(16, ROWS), :]
            tot = jnp.zeros((ROWS, 128), F32)
            for j in range(7):
                row = i * 7 + j
                term = sf[row : row + 1, lanes] * mx[pl.ds(8 - j, ROWS), :]
                tot = tot + (jnp.where(pos >= j, term, 0.0) if j else term)
            out[:, lanes] = (g * tot).astype(BF)
            return carry
        lax.fori_loop(0, 4, unit, 0)

    def long_features():
        def unit(lt, carry):
            lanes = lanes_of(lt)
            g, mixed = features(2, lanes)
            gate[:, lanes] = g
            ml[:, lanes] = mixed[8:]
            msend[:, lanes] = mixed[16:].astype(BF)
            return carry
        lax.fori_loop(0, 4, unit, 0)

    mcopy = rcopy(msend, rimm, mssem.at[0], mrsem.at[0], ctx=nxt)

    def long_filters():
        taps = lfb[...].reshape(128, 256)
        sel = (iota((32, 256), 1) == 32 * ch + iota((32, 256), 0)).astype(BF)
        cg[...] = lax.dot_general(sel, taps, (((1,), (1,)), ((), ())), preferred_element_type=F32)
        selc = (iota((256, 512), 0) == 32 * ch + (iota((256, 512), 1) >> 4)).astype(BF)
        wide = jnp.dot(taps, selc, preferred_element_type=F32).astype(BF)
        rev = (iota((128, 128), 0) + iota((128, 128), 1) == 127).astype(BF)
        erev[...] = jnp.dot(rev, wide, preferred_element_type=F32)

    def long_conv():
        prow = pv[0, 0:1, 0:128]
        pi, ti = iota((128, 128), 0), iota((128, 128), 1)
        top = ((ti < pi) & (ti + 128 - pi <= prow)).astype(F32)
        bot = ((ti >= pi) & (ti - pi <= prow)).astype(F32)

        def unit(lt, carry):
            lanes = lanes_of(lt)
            rm = jnp.where(me > 0, rimm[:, lanes].astype(F32), 0.0)
            loc_m = ml[:, lanes]
            mx2[pl.ds(0, 128), :] = rm
            mx2[pl.ds(128, ROWS), :] = loc_m
            mT[:, pl.ds(0, 128)] = rm.T.astype(BF)
            mT[:, pl.ds(128, 128)] = loc_m[:128].T.astype(BF)

            for g in range(8):
                f = jnp.broadcast_to(cg[pl.ds(lt * 8 + g, 1), :], (128, 128))
                r = pltpu.roll(f, 0, 1, stride=1, stride_axis=0)
                tt = jnp.concatenate([(r * top).astype(BF), (r * bot).astype(BF)], axis=0)
                cT[pl.ds(g * 16, 16), :] = jnp.dot(mT[pl.ds(g * 16, 16), :], tt, preferred_element_type=F32)
            conv = cT[...].T
            out2[pl.ds(0, 128), lanes] = (gate[pl.ds(0, 128), lanes] * conv).astype(BF)
            er = erev[:, lanes]
            back = 127 - iota((128, 128), 0)
            rows = []
            for i in range(8):
                pos = posc[pl.ds(144 + i, 1), :]
                term = jnp.where(back <= pos, er * mx2[pl.ds(129 + i, 128), :], 0.0)
                rows.append(jnp.sum(term, axis=0, keepdims=True))
            tail = jnp.concatenate(rows, axis=0)
            out2[pl.ds(128, 8), lanes] = (gate[pl.ds(128, 8), lanes] * tail).astype(BF)
            return carry
        lax.fori_loop(0, 4, unit, 0)

    def forward(s):
        for c in range(2):
            for d in range(2):
                kvwait(d, s, c)
                if d == 0:
                    @pl.when(s < 7)
                    def _():
                        kvcopy(0, s + 1, c).start()
                else:
                    kvcopy(1, s + 1, c).start()

    att([z])

    def step(s, carry):
        forward(s)
        att([(z - s + NZ) % NZ, (z + s) % NZ])

        @pl.when(s == 1)
        def _():
            for i in (2, 0, 1):
                raw[i].wait_recv()
            long_features()
            for c in fs:
                c.wait_recv()

        @pl.when(s == 2)
        def _():
            long_filters()
            mcopy.start()

        @pl.when(s == 3)
        def _():
            short_layer(0, out0)

        @pl.when(s == 4)
        def _():
            short_layer(1, out1)

        @pl.when(s == 5)
        def _():
            mcopy.wait_recv()
            long_conv()

        return carry

    lax.fori_loop(1, 8, step, 0)
    for c in range(2):
        kvwait(1, 8, c)
    att([(z + 8) % NZ])

    auxs[...] = jnp.zeros_like(auxs)
    auxs[0:2, :] = mrow[0:2, :]
    auxs[2:4, :] = lrow[0:2, :]
    aux_copies = [rcopy(auxs, auxr.at[4 - r], asend.at[r - 1], arecv.at[3 - r], ctx=ydev(r)) for r in range(1, 4)]
    for h in range(2):
        for k in range(5):
            of32[pl.ds(k * 128, 128), pl.ds(h * HD, HD)] = acc[h, :, pl.ds(k * 128, 128)].T
    for r in range(1, 4):
        ob[r - 1] = of32[pl.ds(ROWS * r, ROWS), :].astype(BF)
    o_copies = [rcopy(ob.at[r - 1], orecv.at[3 - r], osend.at[r - 1], osrecv.at[3 - r], ctx=ydev(r)) for r in range(1, 4)]
    for c in aux_copies + o_copies:
        c.start()
    for c in aux_copies:
        c.wait_recv()
    ms, ls = [auxs[0:2, 0:256]], [auxs[2:4, 0:256]]
    for k in range(1, 4):
        shifted = pltpu.roll(auxr[k], QW - ROWS * (4 - k), 1)[:, 0:256]
        ms.append(shifted[0:2])
        ls.append(shifted[2:4])
    top_m = functools.reduce(jnp.maximum, ms)
    es = [jnp.exp2((m - top_m) * COEF) for m in ms]
    den = functools.reduce(jnp.add, [e * l for e, l in zip(es, ls)])
    den = jnp.where(den > 0, den, 1.0)
    ws = jnp.concatenate([e / den for e in es] + [jnp.zeros((120, 256), F32)], axis=0)
    wt = jnp.concatenate([ws[:, :128].T, ws[:, 128:].T], axis=0)[:ROWS]
    for c in o_copies:
        c.wait_recv()
    for h in range(2):
        hs = pl.ds(h * HD, HD)
        tot = of32[pl.ds(0, ROWS), hs] * wt[:, h : h + 1]
        for k in range(1, 4):
            tot = tot + orecv[k - 1, :, hs].astype(F32) * wt[:, 2 * k + h : 2 * k + h + 1]
        attn[:, hs] = tot.astype(BF)

    for c in raw + qs + ps + fs + [mcopy] + aux_copies + o_copies:
        c.wait_send()
    for s in range(1, 9):
        for c in range(2):
            for d in range(2):
                if d == 1 or s < 8:
                    kvcopy(d, s, c).wait_send()


def body(attn_proj, first_in, second_in, third_in, feat_filters, short_filters, long_filter, positions):
    t3 = lambda v: jnp.transpose(v, (1, 0, 2))
    wf = jnp.pad(feat_filters.reshape(27, 512).astype(F32), ((0, 5), (0, 0)))
    sf = jnp.pad(jnp.repeat(short_filters.astype(F32).reshape(14, 32), 16, axis=1), ((0, 2), (0, 0)))
    posl = jnp.stack(
        [jnp.broadcast_to(jnp.pad(positions, (ROWS * r, QW - ROWS * (r + 1)))[None], (8, QW)) for r in range(4)]
    )
    ext = jnp.concatenate([positions[0] + jnp.arange(-16, 0, dtype=jnp.int32), positions])
    posc = jnp.broadcast_to(ext[:, None], (152, 128))
    vm = pl.BlockSpec(memory_space=pltpu.VMEM)
    hbm = pl.BlockSpec(memory_space=pl.ANY)
    dma = pltpu.SemaphoreType.DMA
    v = pltpu.VMEM
    return pl.pallas_call(
        kernel,
        out_shape=(
            jax.ShapeDtypeStruct((ROWS, 256), BF),
            jax.ShapeDtypeStruct((ROWS, 512), BF),
            jax.ShapeDtypeStruct((ROWS, 512), BF),
            jax.ShapeDtypeStruct((ROWS, 512), BF),
        ),
        in_specs=[hbm, hbm, hbm, hbm, vm, vm, hbm, hbm, vm],
        out_specs=[vm] * 4,
        scratch_shapes=[
            v((4, ROWS, 256), BF),
            v((NZ, 2, ROWS, 256), BF),
            v((4, 8, QW), jnp.int32),
            v((3, 3, ROWS, 512), BF),
            v((3, 3, 8, 512), BF),
            v((8, 16, 256), BF),
            v((3, 152, 128), F32),
            v((144, 128), F32),
            v((264, 128), F32),
            v((ROWS, 512), F32),
            v((ROWS, 512), F32),
            v((128, 512), BF),
            v((128, 512), BF),
            v((128, 256), BF),
            v((128, 128), F32),
            v((32, 128), F32),
            v((128, 512), F32),
            v((QW, 256), BF),
            v((2, HD, QW), F32),
            v((8, QW), F32),
            v((8, QW), F32),
            v((8, QW), jnp.int32),
            v((8, QW), jnp.int32),
            v((QW, 256), F32),
            v((3, ROWS, 256), BF),
            v((3, ROWS, 256), BF),
            v((8, QW), F32),
            v((4, 8, QW), F32),
            dma((7,)),
            dma((2, 8, 2)),
            dma((2, 8, 2)),
            dma((3,)),
            dma((3,)),
            dma((3,)),
            dma((3,)),
            dma((3,)),
            dma((3,)),
            dma((7,)),
            dma((7,)),
            dma((1,)),
            dma((1,)),
            dma((3,)),
            dma((3,)),
            dma((3,)),
            dma((3,)),
        ],
        compiler_params=pltpu.CompilerParams(collective_id=0, has_side_effects=True, vmem_limit_bytes=48 << 20),
        name="mixer",
    )(t3(attn_proj), t3(first_in), t3(second_in), t3(third_in), wf, sf, long_filter, posl, posc)


def solution(mesh):
    in_specs = (
        P("ctx", None, "ch"),
        P("ctx", None, "ch"),
        P("ctx", None, "ch"),
        P("ctx", None, "ch"),
        P(None, None, None, "ch"),
        P(None, None, "ch"),
        P("ch", None),
        P("ctx"),
    )
    out_specs = (P("ctx", "ch"), P("ctx", "ch"), P("ctx", "ch"), P("ctx", "ch"))
    return jax.shard_map(body, mesh=mesh, in_specs=in_specs, out_specs=out_specs, check_vma=False)
```

```python
import functools
import math

import jax
import jax.numpy as jnp
from jax import lax
from jax.experimental import pallas as pl
from jax.experimental.pallas import tpu as pltpu
from jax.sharding import PartitionSpec as P

NY, NZ, NCH = 4, 16, 8
ROWS = 136
HD = 128
QW = 640
COEF = math.log2(math.e) / math.sqrt(HD)
MESH = pl.DeviceIdType.MESH
BF, F32 = jnp.bfloat16, jnp.float32
TILES = ((0, 256), (256, 256), (512, 128))


def iota(shape, dim):
    return lax.broadcasted_iota(jnp.int32, shape, dim)


def kernel(
    qkv, x0, x1, x2, wf, sfr, lf, posr,
    attn, out0, out1, out2,
    qb, kv, pv, xv, rim, lfb, xf, mx, mx2, gate, ml, msend, rimm, mT, cT, cg, erev,
    qall, acc, mrow, lrow, tq, ds, of32, ob, orecv, auxs, auxr, posl, posc, sf, sfs,
    loc, ksend, krecv, qsend, qrecv, psend, precv, rsend, rrecv, fsend, frecv,
    mssem, mrsem, osend, osrecv, asend, arecv,
):
    me = lax.axis_index("ctx")
    ch = lax.axis_index("ch")
    y, z = me // NZ, me % NZ
    xs = (x0, x1, x2)

    def zdev(k):
        return y * NZ + (z + k + NZ) % NZ

    def ydev(k):
        return ((y + k) % NY) * NZ + z

    nxt, prv = (me + 1) % (NY * NZ), (me + NY * NZ - 1) % (NY * NZ)

    def rcopy(src, dst, ss, rs, **dev):
        return pltpu.make_async_remote_copy(
            src_ref=src, dst_ref=dst, send_sem=ss, recv_sem=rs, device_id=dev, device_id_type=MESH
        )

    locals_ = [
        pltpu.make_async_copy(qkv.at[1 + c, :, pl.ds(h * HD, HD)], kv.at[z, c, h], loc.at[2 * c + h])
        for c in range(2)
        for h in range(2)
    ]
    locals_ += [
        pltpu.make_async_copy(qkv.at[0], qb.at[0], loc.at[4]),
        pltpu.make_async_copy(lf, lfb.at[ch], loc.at[5]),
    ]
    locals_ += [pltpu.make_async_copy(xs[i], xv.at[i], loc.at[6 + i]) for i in range(3)]
    for c in locals_:
        c.start()

    bar = pltpu.get_barrier_semaphore()
    peers = [zdev(1), zdev(-1), ydev(1), ydev(2), ydev(3), nxt, prv]
    for p in peers:
        pl.semaphore_signal(bar, inc=1, device_id={"ctx": p}, device_id_type=MESH)
    for d in range(1, NCH):
        pl.semaphore_signal(bar, inc=1, device_id={"ch": (ch + d) % NCH}, device_id_type=MESH)

    own = jnp.concatenate([posr[...].astype(F32), jnp.zeros((1, QW - ROWS), F32)], axis=1)
    wide_pos = jnp.broadcast_to(own, (8, QW))
    for r in range(4):
        posl[r] = (pltpu.roll(wide_pos, ROWS * r, 1) if r else wide_pos)[0:1]
    head = jnp.broadcast_to(own[:, 0:128], (128, 128)).T
    posc[pl.ds(16, 128), :] = head
    posc[pl.ds(144, 8), :] = jnp.broadcast_to(own[:, 128:256], (128, 128)).T[0:8]
    posc[pl.ds(8, 8), :] = head[0:1] + (iota((8, 128), 0) - 8).astype(F32)
    sfs[...] = jnp.zeros_like(sfs)
    for j in range(7):
        sfs[pl.ds(j, 1), :] = sfr[j, 0:1, :].astype(F32)
        sfs[pl.ds(8 + j, 1), :] = sfr[j, 1:2, :].astype(F32)
    spread = (iota((32, 512), 0) == (iota((32, 512), 1) >> 4)).astype(BF)
    sf[...] = jnp.dot(sfs[...].astype(BF), spread, preferred_element_type=F32)
    acc[...] = jnp.zeros_like(acc)
    mrow[...] = jnp.full_like(mrow, -1e20)
    lrow[...] = jnp.zeros_like(lrow)
    pl.semaphore_wait(bar, len(peers) + NCH - 1)

    def part(blk, c):
        return kv.at[blk, c // 2, c % 2]

    def kvcopy(d, s, c):
        blk = (z - s + 1 + NZ) % NZ if d == 0 else (z + s - 1) % NZ
        tgt = zdev(1) if d == 0 else zdev(-1)
        return rcopy(part(blk, c), part(blk, c), ksend.at[d, s - 1, c], krecv.at[d, s - 1, c], ctx=tgt)

    def kvwait(d, s, c):
        blk = (z - s + NZ) % NZ if d == 0 else (z + s) % NZ
        rcopy(part(blk, c), part(blk, c), ksend.at[d, s - 1, c], krecv.at[d, s - 1, c], ctx=prv).wait_recv()

    for c in range(4):
        locals_[c].wait()
        for d in range(2):
            kvcopy(d, 1, c).start()
    raw = [rcopy(xs[i].at[:, pl.ds(128, 8), :], rim.at[i], rsend.at[i], rrecv.at[i], ctx=nxt) for i in range(3)]
    for i in (2, 0, 1):
        raw[i].start()
    locals_[4].wait()
    locals_[5].wait()
    qs = [rcopy(qb.at[0], qb.at[r], qsend.at[r - 1], qrecv.at[r - 1], ctx=ydev(4 - r)) for r in range(1, 4)]
    ps = [rcopy(posl.at[r], pv.at[r - 1], psend.at[r - 1], precv.at[r - 1], ctx=ydev(4 - r)) for r in range(1, 4)]
    fs = [
        rcopy(lfb.at[ch], lfb.at[ch], fsend.at[d - 1], frecv.at[d - 1], ch=(ch + d) % NCH)
        for d in range(1, NCH)
    ]
    for c in qs + ps + fs:
        c.start()
    for i in range(3):
        locals_[6 + i].wait()

    for c in qs + ps:
        c.wait_recv()
    lane = iota((8, QW), 1)
    b = (
        (lane >= ROWS).astype(jnp.int32)
        + (lane >= 2 * ROWS).astype(jnp.int32)
        + (lane >= 3 * ROWS).astype(jnp.int32)
    )
    yq = (y + b) % NY
    t_all = (yq * NZ + z) * ROWS + lane - ROWS * b
    tq[...] = t_all
    all_pos = posl[0] + pv[0] + pv[1] + pv[2]
    ds[...] = t_all - jnp.broadcast_to(all_pos, (8, QW)).astype(jnp.int32)
    of32[pl.ds(544, 96), :] = jnp.zeros((96, 256), F32)
    for r in range(4):
        of32[pl.ds(ROWS * r, ROWS), :] = qb[r].astype(F32)
    qall[...] = of32[...].astype(BF)

    def att(blocks):
        for h in range(2):
            hs = pl.ds(h * HD, HD)
            ks = [kv[blk, 0, h] for blk in blocks]
            vs = [kv[blk, 1, h] for blk in blocks]
            for lo, w in TILES:
                cs = pl.ds(lo, w)
                q = qall[cs, hs]
                t_row, d_row = tq[0:1, cs], ds[0:1, cs]
                scores = []
                m_old = mrow[h : h + 1, cs]
                m_new = m_old
                for blk, k in zip(blocks, ks):
                    s = lax.dot_general(k, q, (((1,), (1,)), ((), ())), preferred_element_type=F32)
                    kid = (y * NZ + blk) * ROWS + iota((ROWS, w), 0)
                    s = jnp.where((kid <= t_row) & (kid >= d_row), s, -1e30)
                    scores.append(s)
                    m_new = jnp.maximum(m_new, jnp.max(s, axis=0, keepdims=True))
                alpha = jnp.exp2((m_old - m_new) * COEF)
                l_new = lrow[h : h + 1, cs] * alpha
                o_new = acc[h, :, cs] * alpha
                for s, v in zip(scores, vs):
                    p = jnp.exp2((s - m_new) * COEF)
                    l_new = l_new + jnp.sum(p, axis=0, keepdims=True)
                    o_new = o_new + lax.dot_general(
                        v, p.astype(BF), (((0,), (0,)), ((), ())), preferred_element_type=F32
                    )
                mrow[h : h + 1, cs] = m_new
                lrow[h : h + 1, cs] = l_new
                acc[h, :, cs] = o_new

    def features(i, lanes):
        out = []
        pos = posc[pl.ds(8, 144), :]
        for a in range(3):
            xf[a, pl.ds(0, 8), :] = jnp.zeros((8, 128), F32)
            xf[a, pl.ds(8, 8), :] = jnp.where(me > 0, rim[i, a, :, lanes].astype(F32), 0.0)
            xf[a, pl.ds(16, ROWS), :] = xv[i, a, :, lanes].astype(F32)
            tot = jnp.zeros((144, 128), F32)
            for j in range(3):
                term = wf[i, j, a : a + 1, lanes].astype(F32) * xf[a, pl.ds(8 - j, 144), :]
                tot = tot + (jnp.where(pos >= j, term, 0.0) if j else term)
            out.append(tot)
        mixed = (out[1] * out[2]).astype(BF).astype(F32)
        return out[0][8:], mixed

    def lanes_of(lt):
        return pl.ds(pl.multiple_of(lt * 128, 128), 128)

    def short_layer(i, out):
        def unit(lt, carry):
            lanes = lanes_of(lt)
            g, mixed = features(i, lanes)
            mx[...] = mixed
            pos = posc[pl.ds(16, ROWS), :]
            tot = jnp.zeros((ROWS, 128), F32)
            for j in range(7):
                row = i * 8 + j
                term = sf[row : row + 1, lanes] * mx[pl.ds(8 - j, ROWS), :]
                tot = tot + (jnp.where(pos >= j, term, 0.0) if j else term)
            out[:, lanes] = (g * tot).astype(BF)
            return carry
        lax.fori_loop(0, 4, unit, 0)

    def long_features():
        def unit(lt, carry):
            lanes = lanes_of(lt)
            g, mixed = features(2, lanes)
            gate[:, lanes] = g
            ml[:, lanes] = mixed[8:]
            msend[:, lanes] = mixed[16:].astype(BF)
            return carry
        lax.fori_loop(0, 4, unit, 0)

    mcopy = rcopy(msend, rimm, mssem.at[0], mrsem.at[0], ctx=nxt)

    def long_filters():
        taps = lfb[...].reshape(128, 256)
        sel = (iota((32, 256), 1) == 32 * ch + iota((32, 256), 0)).astype(BF)
        cg[...] = lax.dot_general(sel, taps, (((1,), (1,)), ((), ())), preferred_element_type=F32)
        selc = (iota((256, 512), 0) == 32 * ch + (iota((256, 512), 1) >> 4)).astype(BF)
        wide = jnp.dot(taps, selc, preferred_element_type=F32).astype(BF)
        rev = (iota((128, 128), 0) + iota((128, 128), 1) == 127).astype(BF)
        erev[...] = jnp.dot(rev, wide, preferred_element_type=F32)

    def long_conv():
        prow = posl[0, 0:1, 0:128]
        pi, ti = iota((128, 128), 0), iota((128, 128), 1)
        top = ((ti < pi) & ((ti + 128 - pi).astype(F32) <= prow)).astype(F32)
        bot = ((ti >= pi) & ((ti - pi).astype(F32) <= prow)).astype(F32)

        def unit(lt, carry):
            lanes = lanes_of(lt)
            rm = jnp.where(me > 0, rimm[:, lanes].astype(F32), 0.0)
            loc_m = ml[:, lanes]
            mx2[pl.ds(0, 128), :] = rm
            mx2[pl.ds(128, ROWS), :] = loc_m
            mT[:, pl.ds(0, 128)] = rm.T.astype(BF)
            mT[:, pl.ds(128, 128)] = loc_m[:128].T.astype(BF)

            for g in range(8):
                f = jnp.broadcast_to(cg[pl.ds(lt * 8 + g, 1), :], (128, 128))
                r = pltpu.roll(f, 0, 1, stride=1, stride_axis=0)
                tt = jnp.concatenate([(r * top).astype(BF), (r * bot).astype(BF)], axis=0)
                cT[pl.ds(g * 16, 16), :] = jnp.dot(mT[pl.ds(g * 16, 16), :], tt, preferred_element_type=F32)
            conv = cT[...].T
            out2[pl.ds(0, 128), lanes] = (gate[pl.ds(0, 128), lanes] * conv).astype(BF)
            er = erev[:, lanes]
            back = (127 - iota((128, 128), 0)).astype(F32)
            rows = []
            for i in range(8):
                pos = posc[pl.ds(144 + i, 1), :]
                term = jnp.where(back <= pos, er * mx2[pl.ds(129 + i, 128), :], 0.0)
                rows.append(jnp.sum(term, axis=0, keepdims=True))
            tail = jnp.concatenate(rows, axis=0)
            out2[pl.ds(128, 8), lanes] = (gate[pl.ds(128, 8), lanes] * tail).astype(BF)
            return carry
        lax.fori_loop(0, 4, unit, 0)

    def forward(s):
        for c in range(4):
            for d in range(2):
                kvwait(d, s, c)
                if d == 0:
                    @pl.when(s < 7)
                    def _():
                        kvcopy(0, s + 1, c).start()
                else:
                    kvcopy(1, s + 1, c).start()

    att([z])

    def step(s, carry):
        forward(s)
        att([(z - s + NZ) % NZ, (z + s) % NZ])

        @pl.when(s == 1)
        def _():
            for i in (2, 0, 1):
                raw[i].wait_recv()
            long_features()
            for c in fs:
                c.wait_recv()

        @pl.when(s == 2)
        def _():
            long_filters()
            mcopy.start()

        @pl.when(s == 3)
        def _():
            short_layer(0, out0)

        @pl.when(s == 4)
        def _():
            short_layer(1, out1)

        @pl.when(s == 5)
        def _():
            mcopy.wait_recv()
            long_conv()

        return carry

    lax.fori_loop(1, 8, step, 0)
    for c in range(4):
        kvwait(1, 8, c)
    att([(z + 8) % NZ])

    both = jnp.concatenate([mrow[0:2, :], lrow[0:2, :], jnp.zeros((4, QW), F32)], axis=0)
    for r in range(1, 4):
        auxs[r - 1] = pltpu.roll(both, QW - ROWS * r, 1)[:, 0:256]
    aux_copies = [
        rcopy(auxs.at[r - 1], auxr.at[3 - r], asend.at[r - 1], arecv.at[3 - r], ctx=ydev(r)) for r in range(1, 4)
    ]
    for h in range(2):
        for k in range(5):
            of32[pl.ds(k * 128, 128), pl.ds(h * HD, HD)] = acc[h, :, pl.ds(k * 128, 128)].T
    for r in range(1, 4):
        ob[r - 1] = of32[pl.ds(ROWS * r, ROWS), :].astype(BF)
    o_copies = [rcopy(ob.at[r - 1], orecv.at[3 - r], osend.at[r - 1], osrecv.at[3 - r], ctx=ydev(r)) for r in range(1, 4)]
    for c in aux_copies + o_copies:
        c.start()
    for c in aux_copies:
        c.wait_recv()
    ms, ls = [both[0:2, 0:256]], [both[2:4, 0:256]]
    for k in range(1, 4):
        ms.append(auxr[k - 1, 0:2, :])
        ls.append(auxr[k - 1, 2:4, :])
    top_m = functools.reduce(jnp.maximum, ms)
    es = [jnp.exp2((m - top_m) * COEF) for m in ms]
    den = functools.reduce(jnp.add, [e * l for e, l in zip(es, ls)])
    den = jnp.where(den > 0, den, 1.0)
    ws = jnp.concatenate([e / den for e in es] + [jnp.zeros((120, 256), F32)], axis=0)
    wt = jnp.concatenate([ws[:, :128].T, ws[:, 128:].T], axis=0)[:ROWS]
    for c in o_copies:
        c.wait_recv()
    for h in range(2):
        hs = pl.ds(h * HD, HD)
        tot = of32[pl.ds(0, ROWS), hs] * wt[:, h : h + 1]
        for k in range(1, 4):
            tot = tot + orecv[k - 1, :, hs].astype(F32) * wt[:, 2 * k + h : 2 * k + h + 1]
        attn[:, hs] = tot.astype(BF)

    for c in raw + qs + ps + fs + [mcopy] + aux_copies + o_copies:
        c.wait_send()
    for s in range(1, 9):
        for c in range(4):
            for d in range(2):
                if d == 1 or s < 8:
                    kvcopy(d, s, c).wait_send()


def finish(outs):
    def place(*refs):
        sems = refs[8]
        copies = [pltpu.make_async_copy(refs[i], refs[4 + i], sems.at[i]) for i in range(4)]
        for c in copies:
            c.start()
        for c in copies:
            c.wait()

    return pl.pallas_call(
        place,
        out_shape=tuple(jax.ShapeDtypeStruct(o.shape, o.dtype) for o in outs),
        in_specs=[pl.BlockSpec(memory_space=pltpu.VMEM)] * 4,
        out_specs=[pl.BlockSpec(memory_space=pltpu.HBM)] * 4,
        scratch_shapes=[pltpu.SemaphoreType.DMA((4,))],
        compiler_params=pltpu.CompilerParams(vmem_limit_bytes=1 << 20),
        name="finish",
    )(*outs)


def body(attn_proj, first_in, second_in, third_in, feat_filters, short_filters, long_filter, positions):
    t3 = lambda v: jnp.transpose(v, (1, 0, 2))
    vm = pl.BlockSpec(memory_space=pltpu.VMEM)
    hbm = pl.BlockSpec(memory_space=pltpu.HBM)
    dma = pltpu.SemaphoreType.DMA
    v = pltpu.VMEM
    outs = pl.pallas_call(
        kernel,
        out_shape=(v((ROWS, 256), BF), v((ROWS, 512), BF), v((ROWS, 512), BF), v((ROWS, 512), BF)),
        in_specs=[hbm, hbm, hbm, hbm, vm, vm, hbm, vm],
        out_specs=[vm] * 4,
        scratch_shapes=[
            v((4, ROWS, 256), BF),
            v((NZ, 2, 2, ROWS, HD), BF),
            v((3, 1, QW), F32),
            v((3, 3, ROWS, 512), BF),
            v((3, 3, 8, 512), BF),
            v((8, 16, 256), BF),
            v((3, 152, 128), F32),
            v((144, 128), F32),
            v((264, 128), F32),
            v((ROWS, 512), F32),
            v((ROWS, 512), F32),
            v((128, 512), BF),
            v((128, 512), BF),
            v((128, 256), BF),
            v((128, 128), F32),
            v((32, 128), F32),
            v((128, 512), F32),
            v((QW, 256), BF),
            v((2, HD, QW), F32),
            v((8, QW), F32),
            v((8, QW), F32),
            v((8, QW), jnp.int32),
            v((8, QW), jnp.int32),
            v((QW, 256), F32),
            v((3, ROWS, 256), BF),
            v((3, ROWS, 256), BF),
            v((3, 8, 256), F32),
            v((3, 8, 256), F32),
            v((4, 1, QW), F32),
            v((152, 128), F32),
            v((16, 512), F32),
            v((16, 32), F32),
            dma((9,)),
            dma((2, 8, 4)),
            dma((2, 8, 4)),
            dma((3,)),
            dma((3,)),
            dma((3,)),
            dma((3,)),
            dma((3,)),
            dma((3,)),
            dma((7,)),
            dma((7,)),
            dma((1,)),
            dma((1,)),
            dma((3,)),
            dma((3,)),
            dma((3,)),
            dma((3,)),
        ],
        compiler_params=pltpu.CompilerParams(collective_id=0, has_side_effects=True, vmem_limit_bytes=60_000_000),
        name="mixer",
    )(t3(attn_proj), t3(first_in), t3(second_in), t3(third_in), feat_filters, t3(short_filters), long_filter, positions.reshape(1, ROWS))
    return finish(outs)


def solution(mesh):
    in_specs = (
        P("ctx", None, "ch"),
        P("ctx", None, "ch"),
        P("ctx", None, "ch"),
        P("ctx", None, "ch"),
        P(None, None, None, "ch"),
        P(None, None, "ch"),
        P("ch", None),
        P("ctx"),
    )
    out_specs = (P("ctx", "ch"), P("ctx", "ch"), P("ctx", "ch"), P("ctx", "ch"))
    return jax.shard_map(body, mesh=mesh, in_specs=in_specs, out_specs=out_specs, check_vma=False)
```
